32 devices in a mesh: groups: 2 (over x), tensor: 2 (over core), query: 8 (over z, y).
Axes of the slice: x: 2, y: 2, z: 4, core: 2. Of those that a mesh axis runs over, the one named last changes fastest.
Arguments:
- query_tokens: bfloat16 [1024, 1024], P(('groups', 'tensor', 'query')), parts along dimension 0, may hold values from -6 to 6
- ln_gain: float32 [1024], replicated, may hold values from 0.1 to 1.9
- inner_weight: bfloat16 [1024, 65536], P(None, ('tensor', 'query')), may hold values from -0.1875 to 0.1875
- outer_weight: bfloat16 [65536, 1024], P(('tensor', 'query')), may hold values from -0.03125 to 0.03125
- final_gain: float32 [1024], replicated, may hold values from 0.1 to 1.9
- projection: bfloat16 [1024, 128], replicated, may hold values from -0.1875 to 0.1875
- segment_ids: int32 [1024], P('groups'), parts along dimension 0, may hold values from 0 to 31, never falling along the last dimension, each value on 1 to 32 neighbouring positions
- index_vectors: bfloat16 [131072, 128], P(('groups', 'tensor', 'query')), parts along dimension 0, may hold values from -6 to 6
- doc_ids: int32 [131072], P(('groups', 'tensor', 'query')), parts along dimension 0, may hold values from 0 to 127, as said below
Outputs:
- scores: float32 [32, 4096], P(None, ('groups', 'tensor', 'query')), parts along dimension 1
The draws below stay inside these ranges and needn't reach their ends.
There are 2 independent parts, one for each index of `groups`. The reference program is written for one: setup_inputs(seed, part) draws one part's arguments, and reference() takes and returns one part's arrays. A program takes and returns all parts, laid end to end along the dimension named above; an argument that names none is the same for every part. Nothing has to cross between parts.
Inputs may be any that keep to these rules, and one draw needn't show every extreme that they name: `doc_ids`: within each shard of 4096 tokens the slot numbers never fall, start at 0 and leave no slot out up to the shard's largest; some shard uses all 128 slots. `segment_ids`: every query number appears; a query's tokens stand together.
All inputs are finite; a program needn't handle non-finite values.
Results may differ from the reference program's by a relative error of at most 0.0011.
Values may be sent and summed in bfloat16 or wider, within the bound.
No kernel may reach another device: no remote copies, remote signals or barrier semaphores. Data moves between devices by JAX's collectives and lax.ppermute only.
A program may use at most 128 MiB of HBM per device.

```python
import math
import jax
import jax.numpy as jnp
import numpy as np
from jax import lax

D = 1024
FF = 65536
PROJ = 128
QLEN = 32
IDX_DEV = 4096
DOC_DEV = 128
SHARDS = 16
TOKENS = 512
NQ = 32


def shuffle_one(shard_key):
    return jax.random.permutation(shard_key, IDX_DEV - 1)


def draw_doc_ids(key, part):
    key_count, key_pick, key_perm = jax.random.split(jax.random.fold_in(key, 17), 3)
    counts = jax.random.randint(key_count, (SHARDS,), DOC_DEV // 4, DOC_DEV + 1)
    filled = jax.random.randint(key_pick, (), 0, SHARDS)
    counts = jnp.where(jnp.arange(SHARDS) == filled, DOC_DEV, counts)
    shard_keys = jax.random.split(key_perm, SHARDS)
    shuffled = jax.vmap(shuffle_one)(shard_keys)
    boundary = (shuffled < counts[:, None] - 1).astype(jnp.int32)
    document = jnp.concatenate([jnp.zeros((SHARDS, 1), jnp.int32), jnp.cumsum(boundary, axis=1).astype(jnp.int32)], axis=1)
    return document.reshape(SHARDS * IDX_DEV).astype(jnp.int32)


def block_scale(key, shape, pieces, least, high):
    def one(axis_at, parts):
        heights = jax.random.uniform(jax.random.fold_in(jax.random.fold_in(key, 6), axis_at), (parts,), jnp.float32, least / len(pieces), high / len(pieces))
        return jnp.repeat(jnp.exp(heights), shape[axis_at] // parts).reshape((-1,) + (1,) * (len(shape) - axis_at - 1))

    level = one(*pieces[0])
    for cut in pieces[1:]:
        level = level * one(*cut)
    return level


def length_profile(amount, total, bound, slope):
    weights = [(1 << 20) // math.isqrt(standing ** slope) + 1 for standing in range(2, amount + 1)]
    surplus, given = total - bound - (amount - 1), [1] * (amount - 1)
    while surplus > 0:
        free = [i for i in range(amount - 1) if given[i] < bound]
        mass, budget = sum([weights[i] for i in free]), surplus
        for i in free:
            more = min(bound - given[i], max(1, budget * weights[i] // mass), surplus)
            given[i] = given[i] + more
            surplus = surplus - more
    return np.array([bound] + given)


def uneven_parts(stream_key, count, total, limit, lean):
    if count == 2:
        one = jax.random.randint(stream_key, (), max(1, total - limit), min(limit, total - 1) + 1)
        return jnp.stack([one, total - one])
    tallies = jnp.asarray(length_profile(count, total, limit, lean), jnp.int32)
    couples = (count - 1) // 2
    source_of, receiver = tallies[1:1 + 2 * couples:2], tallies[2:2 + 2 * couples:2]
    margin = jnp.minimum(source_of - 1, limit - receiver)
    moved = jax.random.randint(jax.random.fold_in(stream_key, 1), (couples,), 0, 1 << 20) % (margin + 1)
    tallies = tallies.at[1:1 + 2 * couples:2].set(source_of - moved).at[2:2 + 2 * couples:2].set(receiver + moved)
    return tallies[jax.random.permutation(jax.random.fold_in(stream_key, 2), count)]


def normal_values(own_key, shape, scale, limit, cuts=(), kind=jnp.bfloat16):
    level = block_scale(own_key, shape, cuts, -0.22, 0.18) if cuts else 1.0
    values = jax.random.normal(own_key, shape, jnp.float32) * scale * level
    return jnp.minimum(jnp.maximum(values, -limit), limit).astype(kind)


def setup_inputs(seed: int = 0, part: int = 0) -> dict:
    keys = jax.random.split(jax.random.key(seed), 10)
    part_splits = jax.random.split(jax.random.fold_in(keys[9], part), 10)
    return {
        "query_tokens": normal_values(part_splits[0], (TOKENS, D), 1.0, 6.0, ((0, 16),)),
        "ln_gain": jnp.clip(1.0 + 0.18 * jax.random.normal(keys[1], (D,), jnp.float32), 0.1, 1.9),
        "inner_weight": normal_values(keys[2], (D, FF), D ** -0.5, 0.1875, ((1, 16),)),
        "outer_weight": normal_values(keys[3], (FF, D), (FF // 2) ** -0.5, 0.03125, ((0, 16),)),
        "final_gain": jnp.clip(1.0 + 0.18 * jax.random.normal(keys[4], (D,), jnp.float32), 0.1, 1.9),
        "projection": normal_values(keys[5], (D, PROJ), D ** -0.5, 0.1875),
        "segment_ids": jnp.searchsorted(jnp.cumsum(uneven_parts(part_splits[6], NQ, TOKENS, QLEN, 2)), jnp.arange(TOKENS), side="right").astype(jnp.int32),
        "index_vectors": normal_values(part_splits[7], (SHARDS * IDX_DEV, PROJ), 1.0, 6.0, ((0, 16),)),
        "doc_ids": draw_doc_ids(jax.random.fold_in(jax.random.fold_in(keys[9], part), 71), part),
    }


EPSILON = 1e-06

def rms_rows(values, gain):
    mean_square = lax.optimization_barrier(jnp.mean(values * values, axis=-1, keepdims=True))
    return values * lax.rsqrt(mean_square + EPSILON) * gain

def unit_rows(projected):
    return projected * lax.rsqrt(lax.optimization_barrier(jnp.sum(projected * projected, axis=-1, keepdims=True)) + EPSILON)

def reference(query_tokens, ln_gain, inner_weight, outer_weight, final_gain, projection, segment_ids, index_vectors, doc_ids):
    inputs = query_tokens.astype(jnp.float32)
    normed = rms_rows(inputs, ln_gain.astype(jnp.float32)).astype(jnp.bfloat16)
    block_width = FF // 8
    inner_blocks = inner_weight.reshape(D, 8, block_width).transpose(1, 0, 2)
    outer_blocks = outer_weight.reshape(8, block_width, D)

    def add_block(running, weights):
        hidden = jnp.maximum(jnp.dot(normed, weights[0], preferred_element_type=jnp.float32), 0.0).astype(jnp.bfloat16)
        return (running + jnp.dot(hidden, weights[1], preferred_element_type=jnp.float32), None)
    ff_out, unused = lax.scan(add_block, jnp.zeros((TOKENS, D), jnp.float32), (inner_blocks, outer_blocks))
    mixed = inputs + ff_out
    final = rms_rows(mixed, final_gain.astype(jnp.float32)).astype(jnp.bfloat16)
    vectors = unit_rows(jnp.dot(final, projection, preferred_element_type=jnp.float32)).astype(jnp.bfloat16)
    member = (segment_ids[None, :] == jnp.arange(NQ, dtype=jnp.int32)[:, None]).astype(jnp.float32)
    lengths = lax.optimization_barrier(jnp.sum(member, axis=1))
    shard_vectors = index_vectors.reshape(SHARDS, IDX_DEV, PROJ)
    shard_owners = doc_ids.reshape(SHARDS, IDX_DEV)

    def one_shard(shard):
        sims = jnp.einsum('jp,tp->jt', shard[0].astype(jnp.float32), vectors.astype(jnp.float32))
        best = jax.ops.segment_max(sims, shard[1], num_segments=DOC_DEV)
        present = jnp.any(shard[1][:, None] == jnp.arange(DOC_DEV, dtype=jnp.int32)[None, :], axis=0)
        best = jnp.where(present[:, None], best, 0.0)
        return jnp.einsum('qt,dt->qd', member, best, precision=lax.Precision.HIGHEST)
    per_shard = lax.map(one_shard, (shard_vectors, shard_owners))
    scores = per_shard.transpose(1, 0, 2).reshape(NQ, SHARDS * DOC_DEV)
    return scores / lengths[:, None]
```

```python
import functools

import jax
import jax.numpy as jnp
from jax import lax
from jax.experimental import pallas as pl
from jax.experimental.pallas import tpu as pltpu
from jax.sharding import PartitionSpec as P

DOC_DEV = 128
EPSILON = 1e-06
RING = ("tensor", "query")
LOW = float("-inf")
VMEM = pl.BlockSpec(memory_space=pltpu.VMEM)
SMEM = pl.BlockSpec(memory_space=pltpu.SMEM)


def masks_of(cores, places):
    near = 2 if places % 2 == 0 else 1
    far = [k * near for k in range(places // near)]
    side = [0, 1] if near == 2 else [0]
    core = [c * places for c in range(cores)]
    return far, side, core


def hop(value, mask, count):
    return lax.ppermute(value, RING, [(i, i ^ mask) for i in range(count)])


def gather_rows(rows, far, side, core, count):
    for masks in (far, side, core):
        rows = jnp.concatenate([rows] + [hop(rows, m, count) for m in masks[1:]], axis=0)
    return rows


def norm_kernel(x_ref, gain_ref, out_ref):
    x = x_ref[...].astype(jnp.float32)
    mean_square = jnp.mean(x * x, axis=-1, keepdims=True)
    out_ref[...] = (x * lax.rsqrt(mean_square + EPSILON) * gain_ref[...]).astype(jnp.bfloat16)


def norm_rows(x, gain):
    return pl.pallas_call(
        norm_kernel, out_shape=jax.ShapeDtypeStruct(x.shape, jnp.bfloat16), in_specs=[VMEM, VMEM], out_specs=VMEM
    )(x, gain[None, :])


def ff_kernel(x_ref, inner_ref, outer_ref, keep_ref, send_ref, sum_ref):
    step = pl.program_id(0)
    hidden = jnp.maximum(jnp.dot(x_ref[...], inner_ref[...], preferred_element_type=jnp.float32), 0.0)
    part = jnp.dot(hidden.astype(jnp.bfloat16), outer_ref[...], preferred_element_type=jnp.float32)

    @pl.when(step == 0)
    def first():
        sum_ref[...] = part

    @pl.when(step > 0)
    def later():
        sum_ref[...] += part

    @pl.when(step == pl.num_programs(0) - 1)
    def last():
        half = keep_ref.shape[0]
        keep_ref[...] = sum_ref[:half, :]
        send_ref[...] = sum_ref[half:, :].astype(jnp.bfloat16)


def feed_forward(x, inner, outer):
    rows, width = x.shape
    units = inner.shape[1]
    tile = min(1024, units)
    half = rows // 2
    return pl.pallas_call(
        ff_kernel,
        grid=(units // tile,),
        in_specs=[
            pl.BlockSpec((rows, width), lambda i: (0, 0)),
            pl.BlockSpec((width, tile), lambda i: (0, i)),
            pl.BlockSpec((tile, width), lambda i: (i, 0)),
        ],
        out_specs=[pl.BlockSpec((half, width), lambda i: (0, 0))] * 2,
        out_shape=[jax.ShapeDtypeStruct((half, width), jnp.float32), jax.ShapeDtypeStruct((half, width), jnp.bfloat16)],
        scratch_shapes=[pltpu.VMEM((rows, width), jnp.float32)],
        compiler_params=pltpu.CompilerParams(vmem_limit_bytes=56 << 20),
        cost_estimate=pl.CostEstimate(
            flops=4 * rows * width * units, bytes_accessed=4 * width * units, transcendentals=0
        ),
    )(x, inner, outer)


def project_kernel(x_ref, own_ref, got_ref, gain_ref, proj_ref, out_ref):
    mixed = x_ref[...].astype(jnp.float32) + own_ref[...]
    for k in range(got_ref.shape[0]):
        mixed = mixed + got_ref[k].astype(jnp.float32)
    mean_square = jnp.mean(mixed * mixed, axis=-1, keepdims=True)
    final = (mixed * lax.rsqrt(mean_square + EPSILON) * gain_ref[...]).astype(jnp.bfloat16)
    p = jnp.dot(final, proj_ref[...], preferred_element_type=jnp.float32)
    out_ref[...] = (p * lax.rsqrt(jnp.sum(p * p, axis=-1, keepdims=True) + EPSILON)).astype(jnp.bfloat16)


def project_rows(x, own, got, gain, projection):
    return pl.pallas_call(
        project_kernel,
        out_shape=jax.ShapeDtypeStruct((x.shape[0], projection.shape[1]), jnp.bfloat16),
        in_specs=[VMEM] * 5,
        out_specs=VMEM,
    )(x, own, got, gain[None, :], projection)


def score_kernel(bounds, q_ref, seg_ref, index_ref, keep_ref, out_ref, run_ref, best_ref):
    docs, tokens, slots, queries = index_ref.shape[0], q_ref.shape[0], best_ref.shape[0], out_ref.shape[0]
    rows = 256 if docs % 256 == 0 else 8
    run_ref[0:8, :] = jnp.full((8, tokens), LOW, jnp.float32)
    q = q_ref[...]

    def tile(i, run):
        base = pl.multiple_of(i * rows, rows)
        sims = lax.dot_general(
            index_ref[pl.ds(base, rows), :], q, (((1,), (1,)), ((), ())), preferred_element_type=jnp.float32
        )
        keep = keep_ref[pl.ds(base, rows), :]
        for g in range(0, rows, 8):
            same = jnp.concatenate([keep[g : g + 8, :]] * (tokens // keep.shape[1]), axis=1)
            run = jnp.maximum(sims[g : g + 8, :], run + same)
            run_ref[pl.ds(base + 8 + g, 8), :] = run
        return run

    lax.fori_loop(0, docs // rows, tile, jnp.full((8, tokens), LOW, jnp.float32))
    sub = lax.broadcasted_iota(jnp.int32, (8, tokens), 0)

    def octet(o, carry):
        lines = []
        for k in range(8):
            start, end = bounds[o * 8 + k], bounds[o * 8 + k + 1]
            last = pl.multiple_of((jnp.maximum(end - 1, 0) // 8) * 8, 8)
            row = sub + last
            now = jnp.where((row >= start) & (row < end), run_ref[pl.ds(last + 8, 8), :], LOW)
            ago = jnp.where((row - 8 >= start) & (row - 8 < end), run_ref[pl.ds(last, 8), :], LOW)
            line = jnp.max(jnp.maximum(now, ago), axis=0, keepdims=True)
            lines.append(jnp.where(end > start, line, 0.0))
        best_ref[pl.ds(pl.multiple_of(o * 8, 8), 8), :] = jnp.concatenate(lines, axis=0)
        return carry

    lax.fori_loop(0, slots // 8, octet, 0)
    member = (lax.broadcasted_iota(jnp.int32, (queries, tokens), 0) == seg_ref[...]).astype(jnp.float32)
    lengths = jnp.sum(member, axis=1, keepdims=True)
    totals = lax.dot_general(
        member,
        best_ref[...],
        (((1,), (1,)), ((), ())),
        precision=lax.Precision.HIGHEST,
        preferred_element_type=jnp.float32,
    )
    out_ref[...] = totals / lengths


def slot_bounds(doc_ids):
    ids = lax.iota(jnp.int32, DOC_DEV + 1)
    return jnp.sum((doc_ids[None, :] < ids[:, None]).astype(jnp.int32), axis=1)


def same_as_before(doc_ids):
    before = jnp.concatenate([jnp.full((8,), -1, jnp.int32), doc_ids[:-8]])
    same = jnp.where(before == doc_ids, 0.0, LOW).astype(jnp.float32)
    return jnp.broadcast_to(same[:, None], (doc_ids.shape[0], 128))


def score_rows(vectors, segments, index_vectors, bounds, same, queries):
    tokens, docs = vectors.shape[0], index_vectors.shape[0]
    block = 512 if tokens % 512 == 0 else tokens
    return pl.pallas_call(
        score_kernel,
        out_shape=jax.ShapeDtypeStruct((queries, DOC_DEV), jnp.float32),
        in_specs=[SMEM, VMEM, VMEM, VMEM, VMEM],
        out_specs=VMEM,
        scratch_shapes=[pltpu.VMEM((docs + 8, tokens), jnp.float32), pltpu.VMEM((DOC_DEV, tokens), jnp.float32)],
        compiler_params=pltpu.CompilerParams(vmem_limit_bytes=56 << 20),
        cost_estimate=pl.CostEstimate(flops=2 * tokens * docs * 128, bytes_accessed=docs * 256, transcendentals=0),
    )(bounds, vectors, segments[None, :], index_vectors, same)


def on_device(
    cores,
    places,
    query_tokens,
    ln_gain,
    inner_weight,
    outer_weight,
    final_gain,
    projection,
    segment_ids,
    index_vectors,
    doc_ids,
):
    count = cores * places
    own = query_tokens.shape[0]
    queries = segment_ids.shape[0] // 16
    far, side, core = masks_of(cores, places)
    order = jnp.array([c ^ s ^ f for c in core for s in side for f in far], jnp.int32)
    bounds = slot_bounds(doc_ids)
    same = same_as_before(doc_ids)
    segments = segment_ids.reshape(count, own)[order ^ lax.axis_index(RING)].reshape(-1)

    normed = gather_rows(norm_rows(query_tokens, ln_gain), far, side, core, count)
    keep, send = feed_forward(normed, inner_weight, outer_weight)
    keep = keep + hop(send, core[1], count).astype(jnp.float32)
    if len(side) == 2:
        half = keep.shape[0] // 2
        keep = keep[:half] + hop(keep[half:].astype(jnp.bfloat16), side[1], count).astype(jnp.float32)
    send = keep[own:].astype(jnp.bfloat16)
    got = jnp.stack([hop(send[k * own : (k + 1) * own], m, count) for k, m in enumerate(far[1:])])
    own_vectors = project_rows(query_tokens, keep[:own], got, final_gain, projection)
    vectors = gather_rows(own_vectors, far, side, core, count)
    return score_rows(vectors, segments, index_vectors, bounds, same, queries)


def solution(mesh):
    return jax.shard_map(
        functools.partial(on_device, mesh.shape["tensor"], mesh.shape["query"]),
        mesh=mesh,
        in_specs=(
            P(("groups", "tensor", "query"), None),
            P(),
            P(None, ("tensor", "query")),
            P(("tensor", "query"), None),
            P(),
            P(),
            P("groups"),
            P(("groups", "tensor", "query"), None),
            P(("groups", "tensor", "query")),
        ),
        out_specs=P(None, ("groups", "tensor", "query")),
        check_vma=False,
    )
```
